256 devices in a mesh: pipe: 8 (over y, core), dp: 32 (over z, x).
Axes of the slice: x: 4, y: 4, z: 8, core: 2. Of those that a mesh axis runs over, the one named last changes fastest.
Arguments:
- queries: bfloat16 [8, 7680, 4096], P('pipe', 'dp'), may hold values from -8 to 8
- out_grad: bfloat16 [8, 7680, 4096], P('pipe', 'dp'), may hold values from -16 to 16
- key_weight: bfloat16 [8, 512, 4096], P('pipe', 'dp'), may hold values from -0.25 to 0.25
- value_weight: bfloat16 [8, 512, 4096], P('pipe', 'dp'), may hold values from -0.25 to 0.25
- encoded: bfloat16 [8, 64, 128, 512], P('pipe', 'dp'), may hold values from -4 to 4
- nb_owner: int32 [8, 192, 2], P('pipe', 'dp'), may hold values from 0 to 31, as said below
- nb_block: int32 [8, 192, 2], P('pipe', 'dp'), may hold values from 0 to 1
Outputs:
- query_grad: bfloat16 [8, 7680, 4096], P('pipe', 'dp')
- encoded_grad: float32 [8, 64, 128, 512], P('pipe', 'dp')
The draws below stay inside these ranges and needn't reach their ends.
Inputs may be any that keep to these rules, and one draw needn't show every extreme that they name: `nb_owner`: the 12 entries of one group of 6 consecutive spans name exactly 11 different owners; two entries of one group that name the same owner name the same block.
All inputs are finite; a program needn't handle non-finite values.
Results may differ from the reference program's by a relative error of at most 0.014.
Values may be sent and summed in bfloat16 or wider, within the bound.
No kernel may reach another device: no remote copies, remote signals or barrier semaphores. Data moves between devices by JAX's collectives and lax.ppermute only.
A program may use at most 128 MiB of HBM per device.

```python
import jax
import jax.numpy as jnp
from jax import lax

D_ENC = 512
HEADS = 32
HEAD_DIM = 128
SPAN = 40
NEIGH = 2
NB_LEN = 128
ATT_DEV = 6
NBLK = 2
HD = 4096
TOKENS = 7680
POOL = 64
N_PIPE = 8
N_DP = 32


def neighbour_lists(key):
    base = jax.random.fold_in(key, 7)
    entries = ATT_DEV * NEIGH
    distinct = min(entries - 1, N_DP)
    holder_index = jnp.arange(N_DP, dtype=jnp.int32)
    popular_selection = jax.random.randint(jax.random.fold_in(base, 1), (N_PIPE, 1, 1), 0, N_DP)
    surplus_popular = jax.random.randint(jax.random.fold_in(base, 2), (N_PIPE, 1, N_DP), 0, 8) == 0
    popular_boost = jnp.where(holder_index == popular_selection, 2 ** 18, jnp.where(surplus_popular, 2 ** 17, 0))
    tiebreak_jitter = jax.random.randint(jax.random.fold_in(base, 3), (N_PIPE, N_DP, N_DP), 0, 2 ** 16)
    holder_rating = (tiebreak_jitter + popular_boost) * N_DP + holder_index
    ignored, chosen = lax.top_k(holder_rating, distinct)
    chosen = chosen.astype(jnp.int32)
    block_picks = jax.random.randint(jax.random.fold_in(base, 4), (N_PIPE, N_DP, N_DP), 0, NBLK)
    chosen_blocks = jnp.take_along_axis(block_picks, chosen, axis=2)
    repeat_index = jnp.arange(entries, dtype=jnp.int32) % distinct
    owners_all = jnp.take(chosen, repeat_index, axis=2)
    blocks_all = jnp.take(chosen_blocks, repeat_index, axis=2)
    shuffle_keys = jax.random.randint(jax.random.fold_in(base, 5), (N_PIPE, N_DP, entries), 0, 2 ** 16)
    shuffle_keys = shuffle_keys * entries + jnp.arange(entries, dtype=jnp.int32)
    shuffle = jnp.argsort(shuffle_keys, axis=2, stable=True)
    owners_all = jnp.take_along_axis(owners_all, shuffle, axis=2)
    blocks_all = jnp.take_along_axis(blocks_all, shuffle, axis=2)
    owners_all = owners_all.reshape(N_PIPE, N_DP * ATT_DEV, NEIGH).astype(jnp.int32)
    blocks_all = blocks_all.reshape(N_PIPE, N_DP * ATT_DEV, NEIGH).astype(jnp.int32)
    return (owners_all, blocks_all)


def draw_nb_owner(key, part):
    return neighbour_lists(key)[0]


def draw_nb_block(key, part):
    return neighbour_lists(key)[1]


def shard_levels(key, shape, split, smallest, largest):
    loudness, own = 1.0, jax.random.fold_in(key, 6)
    for axis_at, shards_of in split:
        heights = jnp.exp(jax.random.uniform(jax.random.fold_in(own, axis_at), (shards_of,), jnp.float32, smallest / len(split), largest / len(split)))
        loudness = loudness * jnp.repeat(heights, shape[axis_at] // shards_of).reshape([-1 if axis == axis_at else 1 for axis in range(len(shape))])
    return loudness


def centred(rng, extent, scale, most, split=(), kind=jnp.bfloat16):
    values = scale * jax.random.normal(rng, extent, jnp.float32)
    if split:
        values = values * shard_levels(rng, extent, split, -0.22, 0.18)
    return jnp.clip(values, -most, most).astype(kind)


def setup_inputs(seed: int = 0) -> dict:
    key_list = jax.random.split(jax.random.key(seed), 8)
    queries = centred(key_list[0], (N_PIPE, TOKENS, HD), 2.0, 8.0, ((0, 8), (1, 32)))
    out_grad = centred(key_list[1], (N_PIPE, TOKENS, HD), 4.0, 16.0, ((0, 8), (1, 32)))
    key_weight = centred(key_list[2], (N_PIPE, D_ENC, HD), D_ENC ** -0.5, 0.25, ((0, 8), (1, 32)))
    value_weight = centred(key_list[3], (N_PIPE, D_ENC, HD), D_ENC ** -0.5, 0.25, ((0, 8), (1, 32)))
    encoded = centred(key_list[4], (N_PIPE, POOL, NB_LEN, D_ENC), 1.0, 4.0, ((0, 8), (1, 32)))
    nb_owner = draw_nb_owner(jax.random.fold_in(key_list[7], 71), 0)
    nb_block = draw_nb_block(jax.random.fold_in(key_list[7], 71), 0)
    return dict(queries=queries, out_grad=out_grad, key_weight=key_weight, value_weight=value_weight, encoded=encoded, nb_owner=nb_owner, nb_block=nb_block)


def device_step(query_rows, incoming, key_full, value_full, encoded_section, owners, blocks):
    f32 = jnp.float32
    score_scale = HEAD_DIM ** -0.5
    absorbed = jnp.einsum("thd,ehd->the", query_rows.astype(f32), key_full.astype(f32)).astype(jnp.bfloat16)
    grad_side = jnp.einsum("thd,ehd->the", incoming.astype(f32), value_full.astype(f32)).astype(jnp.bfloat16)
    row_index = (owners * NBLK + blocks).astype(jnp.int32)
    neighbours = jnp.take(encoded_section, row_index, axis=0).reshape(ATT_DEV, NEIGH * NB_LEN, D_ENC)
    absorbed4 = absorbed.reshape(ATT_DEV, SPAN, HEADS, D_ENC)
    grad_side4 = grad_side.reshape(ATT_DEV, SPAN, HEADS, D_ENC)
    scores = score_scale * jnp.einsum("cthe,cje->cthj", absorbed4.astype(f32), neighbours.astype(f32))
    exp_scores = jnp.exp(scores)
    attn_probs = exp_scores / jnp.sum(exp_scores, axis=-1, keepdims=True)
    probs_low = attn_probs.astype(jnp.bfloat16)
    prob_grad = jnp.einsum("cthe,cje->cthj", grad_side4.astype(f32), neighbours.astype(f32))
    row_delta = jnp.sum(attn_probs * prob_grad, axis=-1, keepdims=True)
    score_grad = (attn_probs * (prob_grad - row_delta)).astype(jnp.bfloat16)
    absorbed_grad = (score_scale * jnp.einsum("cthj,cje->cthe", score_grad.astype(f32), neighbours.astype(f32))).astype(jnp.bfloat16)
    absorbed_grad = absorbed_grad.reshape(ATT_DEV * SPAN, HEADS, D_ENC)
    query_out = jnp.einsum("the,ehd->thd", absorbed_grad.astype(f32), key_full.astype(f32)).astype(jnp.bfloat16)
    entry_grad = score_scale * jnp.einsum("cthj,cthe->cje", score_grad.astype(f32), absorbed4.astype(f32))
    entry_grad = entry_grad + jnp.einsum("cthj,cthe->cje", probs_low.astype(f32), grad_side4.astype(f32))
    entry_grad = entry_grad.reshape(ATT_DEV * NEIGH, NB_LEN * D_ENC)
    return query_out.reshape(ATT_DEV * SPAN, HEADS * HEAD_DIM), entry_grad, row_index


def reference(queries, out_grad, key_weight, value_weight, encoded, nb_owner, nb_block):
    query_list = []
    pool_list = []
    for section in range(N_PIPE):
        incoming_all = out_grad[(section + 1) % N_PIPE]
        key_full = key_weight[section].reshape(D_ENC, HEADS, HEAD_DIM)
        value_full = value_weight[section].reshape(D_ENC, HEADS, HEAD_DIM)
        encoded_section = encoded[section]

        def per_device(running, inputs):
            query_rows, incoming, owners, blocks = inputs
            query_out, entry_grad, row_index = device_step(query_rows, incoming, key_full, value_full, encoded_section, owners, blocks)
            select = (row_index[None, :] == jnp.arange(POOL, dtype=jnp.int32)[:, None]).astype(jnp.float32)
            pool_term = jnp.dot(select, entry_grad, precision=lax.Precision.HIGHEST)
            pool_term = lax.optimization_barrier(pool_term.astype(jnp.bfloat16)).astype(jnp.float32)
            return running + pool_term.reshape(running.shape), query_out

        inputs = (
            queries[section].reshape(N_DP, ATT_DEV * SPAN, HEADS, HEAD_DIM),
            incoming_all.reshape(N_DP, ATT_DEV * SPAN, HEADS, HEAD_DIM),
            nb_owner[section].reshape(N_DP, ATT_DEV * NEIGH).astype(jnp.int32),
            nb_block[section].reshape(N_DP, ATT_DEV * NEIGH).astype(jnp.int32),
        )
        start_grad = jnp.zeros((POOL, NB_LEN, D_ENC), jnp.float32)
        pool_grad, query_portions = lax.scan(per_device, start_grad, inputs)
        query_list.append(query_portions.reshape(TOKENS, HEADS * HEAD_DIM))
        pool_list.append(pool_grad)
    return jnp.stack(query_list), jnp.stack(pool_list)
```

```python
import functools
import jax
import jax.numpy as jnp
from jax import lax
from jax.experimental import pallas as pl
from jax.experimental.pallas import tpu as pltpu
from jax.sharding import PartitionSpec as P

SPAN = 40
HEAD_DIM = 128
SCALE = HEAD_DIM ** (-0.5)
F32 = jnp.float32
BF16 = jnp.bfloat16


def dot(a, b, ca, cb):
    return lax.dot_general(a, b, (((ca,), (cb,)), ((), ())), preferred_element_type=F32)


def scores_kernel(heads, q_ref, g_ref, w_ref, keys_ref, a_ref, b_ref, ds_ref, p_ref):
    spans = a_ref.shape[0]
    enc = a_ref.shape[2]
    key_w = w_ref[:, 0].reshape(enc, heads * HEAD_DIM)
    value_w = w_ref[:, 1].reshape(enc, heads * HEAD_DIM)
    for src, weight, out in ((q_ref, key_w, a_ref), (g_ref, value_w, b_ref)):
        for pair in range(heads // 2):
            wide = []
            for h in (2 * pair, 2 * pair + 1):
                cols = slice(h * HEAD_DIM, (h + 1) * HEAD_DIM)
                wide.append(dot(src[:, cols], weight[:, cols], 1, 1))
            for a in range(spans):
                rows = slice(a * SPAN, (a + 1) * SPAN)
                both = jnp.concatenate([wide[0][rows], wide[1][rows]], axis=0)
                out[a, pair * 2 * SPAN : (pair + 1) * 2 * SPAN, :] = both.astype(BF16)
    for a in range(spans):
        keys = keys_ref[a]
        e = jnp.exp(SCALE * dot(a_ref[a], keys, 1, 1))
        total = jnp.sum(e, axis=-1, keepdims=True)
        guard = jnp.where(total > 1e30, 2.0**-24, 1.0)
        probs = (e * guard) * (1.0 / (total * guard))
        grad = dot(b_ref[a], keys, 1, 1)
        delta = jnp.sum(probs * grad, axis=-1, keepdims=True)
        ds_ref[a] = (probs * (grad - delta)).astype(BF16)
        p_ref[a] = probs.astype(BF16)


def scores_call(q, g, w, keys, groups):
    tok, hd = q.shape
    ranks, _, rows, _ = w.shape
    enc = ranks * rows
    spans, kr, _ = keys.shape
    heads = hd // HEAD_DIM // groups
    m = heads * SPAN
    cols = heads * HEAD_DIM
    return pl.pallas_call(
        functools.partial(scores_kernel, heads),
        grid=(groups,),
        in_specs=[
            pl.BlockSpec((tok, cols), lambda i: (0, i)),
            pl.BlockSpec((tok, cols), lambda i: (0, i)),
            pl.BlockSpec((ranks, 2, rows, cols), lambda i: (0, 0, 0, i)),
            pl.BlockSpec((spans, kr, enc), lambda i: (0, 0, 0)),
        ],
        out_specs=[
            pl.BlockSpec((spans, m, enc), lambda i: (0, i, 0)),
            pl.BlockSpec((spans, m, enc), lambda i: (0, i, 0)),
            pl.BlockSpec((spans, m, kr), lambda i: (0, i, 0)),
            pl.BlockSpec((spans, m, kr), lambda i: (0, i, 0)),
        ],
        out_shape=[
            jax.ShapeDtypeStruct((spans, m * groups, enc), BF16),
            jax.ShapeDtypeStruct((spans, m * groups, enc), BF16),
            jax.ShapeDtypeStruct((spans, m * groups, kr), BF16),
            jax.ShapeDtypeStruct((spans, m * groups, kr), BF16),
        ],
        name="scores",
        cost_estimate=pl.CostEstimate(flops=6 * 10**9, bytes_accessed=40 * 10**6, transcendentals=2 * 10**6),
        compiler_params=pltpu.CompilerParams(vmem_limit_bytes=60 << 20),
    )(q, g, w, keys)


def query_kernel(heads, ds_ref, w_ref, keys_ref, o_ref, wide_ref):
    spans = ds_ref.shape[0]
    enc = keys_ref.shape[2]
    key_w = w_ref[:, 0].reshape(enc, heads * HEAD_DIM)
    for a in range(spans):
        wide = SCALE * dot(ds_ref[a], keys_ref[a], 1, 0)
        for h in range(heads):
            wide_ref[h, a * SPAN : (a + 1) * SPAN, :] = wide[h * SPAN : (h + 1) * SPAN]
    for h in range(heads):
        cols = slice(h * HEAD_DIM, (h + 1) * HEAD_DIM)
        o_ref[:, cols] = dot(wide_ref[h].astype(BF16), key_w[:, cols], 1, 0).astype(BF16)


def query_call(ds, w, keys, groups):
    spans, m_all, kr = ds.shape
    ranks, _, rows, hd = w.shape
    enc = ranks * rows
    heads = hd // HEAD_DIM // groups
    m = heads * SPAN
    cols = heads * HEAD_DIM
    tok = spans * SPAN
    return pl.pallas_call(
        functools.partial(query_kernel, heads),
        grid=(groups,),
        in_specs=[
            pl.BlockSpec((spans, m, kr), lambda i: (0, i, 0)),
            pl.BlockSpec((ranks, 1, rows, cols), lambda i: (0, 0, 0, i)),
            pl.BlockSpec((spans, kr, enc), lambda i: (0, 0, 0)),
        ],
        out_specs=pl.BlockSpec((tok, cols), lambda i: (0, i)),
        out_shape=jax.ShapeDtypeStruct((tok, hd), BF16),
        scratch_shapes=[pltpu.VMEM((heads, tok, enc), F32)],
        name="query_grad",
        cost_estimate=pl.CostEstimate(flops=3 * 10**9, bytes_accessed=12 * 10**6, transcendentals=0),
        compiler_params=pltpu.CompilerParams(vmem_limit_bytes=60 << 20),
    )(ds, w, keys)


def entry_kernel(slot_ref, first_ref, a_ref, b_ref, ds_ref, p_ref, o_ref, sum_ref):
    step = pl.program_id(0)
    rows = o_ref.shape[1]
    per = ds_ref.shape[2] // rows

    @pl.when(step == 0)
    def _():
        o_ref[...] = jnp.zeros_like(o_ref)

    grad = SCALE * dot(ds_ref[0], a_ref[0], 0, 0) + dot(p_ref[0], b_ref[0], 0, 0)
    for n in range(per):
        entry = step * per + n
        first = first_ref[entry]
        part = grad[n * rows : (n + 1) * rows]

        @pl.when(first == entry)
        def _():
            sum_ref[entry] = part

        @pl.when(first != entry)
        def _():
            sum_ref[first] = sum_ref[first] + part

        o_ref[slot_ref[entry]] = sum_ref[first].astype(BF16)


def entry_call(slots, first, a, b, ds, p, n_slots, rows):
    spans, m, enc = a.shape
    kr = ds.shape[2]
    return pl.pallas_call(
        entry_kernel,
        grid_spec=pltpu.PrefetchScalarGridSpec(
            num_scalar_prefetch=2,
            grid=(spans,),
            in_specs=[
                pl.BlockSpec((1, m, enc), lambda i, *_: (i, 0, 0)),
                pl.BlockSpec((1, m, enc), lambda i, *_: (i, 0, 0)),
                pl.BlockSpec((1, m, kr), lambda i, *_: (i, 0, 0)),
                pl.BlockSpec((1, m, kr), lambda i, *_: (i, 0, 0)),
            ],
            out_specs=pl.BlockSpec((n_slots, rows, enc), lambda i, *_: (0, 0, 0)),
            scratch_shapes=[pltpu.VMEM((slots.shape[0], rows, enc), F32)],
        ),
        out_shape=jax.ShapeDtypeStruct((n_slots, rows, enc), BF16),
        name="entry_grad",
        cost_estimate=pl.CostEstimate(flops=4 * 10**9, bytes_accessed=30 * 10**6, transcendentals=0),
        compiler_params=pltpu.CompilerParams(vmem_limit_bytes=60 << 20),
    )(slots, first, a, b, ds, p)


def pick_kernel(where_ref, *refs):
    sources, (out_ref, sem) = refs[:-2], refs[-2:]
    rows = sources[0].shape[1]
    entries = where_ref.shape[0] // 2
    per = out_ref.shape[1] // rows
    for e in range(entries):
        dest = out_ref.at[e // per, pl.ds(e % per * rows, rows)]
        for s, source in enumerate(sources):

            @pl.when(where_ref[2 * e] == s)
            def _():
                pltpu.make_async_copy(source.at[where_ref[2 * e + 1]], dest, sem.at[e]).start()

    for e in range(entries):
        dest = out_ref.at[e // per, pl.ds(e % per * rows, rows)]
        pltpu.make_async_copy(sources[0].at[0], dest, sem.at[e]).wait()


def pick_call(where, sources, spans):
    entries = where.shape[0] // 2
    _, rows, enc = sources[0].shape
    return pl.pallas_call(
        pick_kernel,
        in_specs=[pl.BlockSpec(memory_space=pltpu.SMEM)]
        + [pl.BlockSpec(memory_space=pl.ANY)] * len(sources),
        out_specs=pl.BlockSpec(memory_space=pltpu.VMEM),
        out_shape=jax.ShapeDtypeStruct((spans, entries // spans * rows, enc), BF16),
        scratch_shapes=[pltpu.SemaphoreType.DMA((entries,))],
        name="pick",
        cost_estimate=pl.CostEstimate(flops=0, bytes_accessed=3 * 10**6, transcendentals=0),
    )(where, *sources)


NX = 4


def pairs_x(groups, shift):
    return [(d, d // NX * NX + (d % NX + shift) % NX) for d in range(groups)]


def pairs_z(groups, shift):
    return [(d, (d + shift * NX) % groups) for d in range(groups)]


def shards(queries, out_grad, key_weight, value_weight, encoded, nb_owner, nb_block):
    groups = lax.axis_size("dp")
    nz = groups // NX
    pipe = lax.axis_size("pipe")
    held, rows, enc = encoded.shape[1:]
    owners = nb_owner[0].reshape(-1)
    blocks = nb_block[0].reshape(-1)
    spans = nb_owner.shape[1]
    me = lax.axis_index("dp")

    weights = lax.all_gather(jnp.stack([key_weight[0], value_weight[0]])[None], "dp", axis=0, tiled=True)
    incoming = lax.ppermute(out_grad, "pipe", [(s, (s - 1) % pipe) for s in range(pipe)])[0]

    def send_x(v, shift):
        return lax.ppermute(v, "dp", pairs_x(groups, shift))

    def send_z(v, shift):
        return lax.ppermute(v, "dp", pairs_z(groups, shift))

    own = encoded[0]
    ups, downs = [own], [own]
    for _ in range(nz // 2 - 1):
        ups.append(send_z(ups[-1], 1))
        downs.append(send_z(downs[-1], -1))
    half = held // 2
    far = jnp.concatenate([send_z(ups[-1][:half], 1), send_z(downs[-1][half:], -1)])
    column = jnp.concatenate(ups + [far] + downs[:0:-1])
    mid = column.shape[0] // 2
    right, left = send_x(column, 1), send_x(column, -1)
    sources = [column, right, left, send_x(right[:mid], 1), send_x(left[mid:], -1)]

    apart_z = (me // NX - owners // NX) % nz
    apart_x = (me % NX - owners % NX) % NX
    line = apart_z * held + blocks
    at = jnp.where(
        apart_x == 0, 0, jnp.where(apart_x == 1, 1, jnp.where(apart_x == 3, 2, jnp.where(line < mid, 3, 4)))
    )
    line = jnp.where(at == 4, line - mid, line)
    keys = pick_call(jnp.stack([at, line], axis=1).reshape(-1).astype(jnp.int32), sources, spans)

    a, b, ds, p = scores_call(queries[0], incoming, weights, keys, 4)
    first = jnp.argmax(owners[:, None] == owners[None, :], axis=1).astype(jnp.int32)
    part = entry_call(owners, first, a, b, ds, p, groups, rows)

    match = owners[None, :] == jnp.arange(groups, dtype=jnp.int32)[:, None]
    request = jnp.max(jnp.where(match, blocks[None, :], -1), axis=1)
    wanted = lax.all_to_all(request[:, None], "dp", split_axis=0, concat_axis=0, tiled=True)[:, 0]
    choose = (wanted[:, None] == jnp.arange(held, dtype=jnp.int32)[None, :]).astype(BF16)
    returned = lax.all_to_all(part, "dp", split_axis=0, concat_axis=0, tiled=True)
    query_grad = query_call(ds, weights, keys, 4)
    summed = jnp.dot(choose.T, returned.reshape(groups, -1), preferred_element_type=F32)
    return query_grad[None], summed.reshape(1, held, rows, enc)


def solution(mesh):
    cut = P("pipe", "dp", None)
    deep = P("pipe", "dp", None, None)
    return jax.shard_map(
        shards,
        mesh=mesh,
        in_specs=(cut, cut, cut, cut, deep, cut, cut),
        out_specs=(cut, deep),
        check_vma=False,
    )
```

```python
import functools
import jax
import jax.numpy as jnp
from jax import lax
from jax.experimental import pallas as pl
from jax.experimental.pallas import tpu as pltpu
from jax.sharding import PartitionSpec as P

SPAN = 40
HEAD_DIM = 128
SCALE = HEAD_DIM ** (-0.5)
F32 = jnp.float32
BF16 = jnp.bfloat16


def dot(a, b, ca, cb):
    return lax.dot_general(a, b, (((ca,), (cb,)), ((), ())), preferred_element_type=F32)


def scores_kernel(heads, q_ref, g_ref, w_ref, keys_ref, a_ref, b_ref, ds_ref, p_ref):
    spans = a_ref.shape[0]
    enc = a_ref.shape[2]
    key_w = w_ref[:, 0].reshape(enc, heads * HEAD_DIM)
    value_w = w_ref[:, 1].reshape(enc, heads * HEAD_DIM)
    for src, weight, out in ((q_ref, key_w, a_ref), (g_ref, value_w, b_ref)):
        for pair in range(heads // 2):
            wide = []
            for h in (2 * pair, 2 * pair + 1):
                cols = slice(h * HEAD_DIM, (h + 1) * HEAD_DIM)
                wide.append(dot(src[:, cols], weight[:, cols], 1, 1))
            for a in range(spans):
                rows = slice(a * SPAN, (a + 1) * SPAN)
                both = jnp.concatenate([wide[0][rows], wide[1][rows]], axis=0)
                out[a, pair * 2 * SPAN : (pair + 1) * 2 * SPAN, :] = both.astype(BF16)
    for a in range(spans):
        keys = keys_ref[a]
        e = jnp.exp(SCALE * dot(a_ref[a], keys, 1, 1))
        total = jnp.sum(e, axis=-1, keepdims=True)
        guard = jnp.where(total > 1e30, 2.0**-24, 1.0)
        probs = (e * guard) * (1.0 / (total * guard))
        grad = dot(b_ref[a], keys, 1, 1)
        delta = jnp.sum(probs * grad, axis=-1, keepdims=True)
        ds_ref[a] = (probs * (grad - delta)).astype(BF16)
        p_ref[a] = probs.astype(BF16)


def scores_call(q, g, w, keys, groups):
    tok, hd = q.shape
    ranks, _, rows, _ = w.shape
    enc = ranks * rows
    spans, kr, _ = keys.shape
    heads = hd // HEAD_DIM // groups
    m = heads * SPAN
    cols = heads * HEAD_DIM
    return pl.pallas_call(
        functools.partial(scores_kernel, heads),
        grid=(groups,),
        in_specs=[
            pl.BlockSpec((tok, cols), lambda i: (0, i)),
            pl.BlockSpec((tok, cols), lambda i: (0, i)),
            pl.BlockSpec((ranks, 2, rows, cols), lambda i: (0, 0, 0, i)),
            pl.BlockSpec((spans, kr, enc), lambda i: (0, 0, 0)),
        ],
        out_specs=[
            pl.BlockSpec((spans, m, enc), lambda i: (0, i, 0)),
            pl.BlockSpec((spans, m, enc), lambda i: (0, i, 0)),
            pl.BlockSpec((spans, m, kr), lambda i: (0, i, 0)),
            pl.BlockSpec((spans, m, kr), lambda i: (0, i, 0)),
        ],
        out_shape=[
            jax.ShapeDtypeStruct((spans, m * groups, enc), BF16),
            jax.ShapeDtypeStruct((spans, m * groups, enc), BF16),
            jax.ShapeDtypeStruct((spans, m * groups, kr), BF16),
            jax.ShapeDtypeStruct((spans, m * groups, kr), BF16),
        ],
        name="scores",
        cost_estimate=pl.CostEstimate(flops=6 * 10**9, bytes_accessed=40 * 10**6, transcendentals=2 * 10**6),
        compiler_params=pltpu.CompilerParams(vmem_limit_bytes=60 << 20),
    )(q, g, w, keys)


def query_kernel(heads, ds_ref, w_ref, keys_ref, o_ref, wide_ref):
    spans = ds_ref.shape[0]
    enc = keys_ref.shape[2]
    key_w = w_ref[:, 0].reshape(enc, heads * HEAD_DIM)
    for a in range(spans):
        wide = SCALE * dot(ds_ref[a], keys_ref[a], 1, 0)
        for h in range(heads):
            wide_ref[h, a * SPAN : (a + 1) * SPAN, :] = wide[h * SPAN : (h + 1) * SPAN]
    for h in range(heads):
        cols = slice(h * HEAD_DIM, (h + 1) * HEAD_DIM)
        o_ref[:, cols] = dot(wide_ref[h].astype(BF16), key_w[:, cols], 1, 0).astype(BF16)


def query_call(ds, w, keys, groups):
    spans, _, kr = ds.shape
    ranks, _, rows, hd = w.shape
    enc = ranks * rows
    heads = hd // HEAD_DIM // groups
    m = heads * SPAN
    cols = heads * HEAD_DIM
    tok = spans * SPAN
    return pl.pallas_call(
        functools.partial(query_kernel, heads),
        grid=(groups,),
        in_specs=[
            pl.BlockSpec((spans, m, kr), lambda i: (0, i, 0)),
            pl.BlockSpec((ranks, 1, rows, cols), lambda i: (0, 0, 0, i)),
            pl.BlockSpec((spans, kr, enc), lambda i: (0, 0, 0)),
        ],
        out_specs=pl.BlockSpec((tok, cols), lambda i: (0, i)),
        out_shape=jax.ShapeDtypeStruct((tok, hd), BF16),
        scratch_shapes=[pltpu.VMEM((heads, tok, enc), F32)],
        name="query_grad",
        cost_estimate=pl.CostEstimate(flops=3 * 10**9, bytes_accessed=12 * 10**6, transcendentals=0),
        compiler_params=pltpu.CompilerParams(vmem_limit_bytes=60 << 20),
    )(ds, w, keys)


def entry_kernel(slot_ref, first_ref, a_ref, b_ref, ds_ref, p_ref, o_ref, sum_ref):
    step = pl.program_id(0)
    rows = o_ref.shape[1]
    per = ds_ref.shape[2] // rows

    @pl.when(step == 0)
    def _():
        o_ref[...] = jnp.zeros_like(o_ref)

    grad = SCALE * dot(ds_ref[0], a_ref[0], 0, 0) + dot(p_ref[0], b_ref[0], 0, 0)
    for n in range(per):
        entry = step * per + n
        first = first_ref[entry]
        part = grad[n * rows : (n + 1) * rows]

        @pl.when(first == entry)
        def _():
            sum_ref[entry] = part

        @pl.when(first != entry)
        def _():
            sum_ref[first] = sum_ref[first] + part

        o_ref[slot_ref[entry]] = sum_ref[first].astype(BF16)


def entry_call(slots, first, a, b, ds, p, n_slots, rows, part, parts):
    spans, m, enc = a.shape
    enc = enc // parts
    kr = ds.shape[2]
    return pl.pallas_call(
        entry_kernel,
        grid_spec=pltpu.PrefetchScalarGridSpec(
            num_scalar_prefetch=2,
            grid=(spans,),
            in_specs=[
                pl.BlockSpec((1, m, enc), lambda i, *_: (i, 0, part)),
                pl.BlockSpec((1, m, enc), lambda i, *_: (i, 0, part)),
                pl.BlockSpec((1, m, kr), lambda i, *_: (i, 0, 0)),
                pl.BlockSpec((1, m, kr), lambda i, *_: (i, 0, 0)),
            ],
            out_specs=pl.BlockSpec((n_slots, rows, enc), lambda i, *_: (0, 0, 0)),
            scratch_shapes=[pltpu.VMEM((slots.shape[0], rows, enc), F32)],
        ),
        out_shape=jax.ShapeDtypeStruct((n_slots, rows, enc), BF16),
        name="entry_grad",
        cost_estimate=pl.CostEstimate(flops=4 * 10**9, bytes_accessed=30 * 10**6, transcendentals=0),
        compiler_params=pltpu.CompilerParams(vmem_limit_bytes=60 << 20),
    )(slots, first, a, b, ds, p)


def serve_kernel(table_ref, *refs):
    sources, (out_ref, sem) = refs[:-2], refs[-2:]
    steps = len(sources)
    here = table_ref[out_ref.shape[0]]
    copies = []
    for slot in range(out_ref.shape[0]):
        back = slot % steps
        row = jnp.where(here >= back, here - back, here - back + steps)
        block = jnp.maximum(table_ref[slot // steps * steps + row], 0)
        copies.append(pltpu.make_async_copy(sources[back].at[block], out_ref.at[slot], sem.at[slot]))
        copies[-1].start()
    for copy in copies:
        copy.wait()


def serve_call(table, sources):
    _, rows, enc = sources[0].shape
    slots = table.shape[0] - 1
    return pl.pallas_call(
        serve_kernel,
        in_specs=[pl.BlockSpec(memory_space=pltpu.SMEM)]
        + [pl.BlockSpec(memory_space=pl.ANY)] * len(sources),
        out_specs=pl.BlockSpec(memory_space=pltpu.VMEM),
        out_shape=jax.ShapeDtypeStruct((slots, rows, enc), BF16),
        scratch_shapes=[pltpu.SemaphoreType.DMA((slots,))],
        name="serve",
        cost_estimate=pl.CostEstimate(flops=0, bytes_accessed=8 * 10**6, transcendentals=0),
    )(table, *sources)


def pick_kernel(slot_ref, source_ref, out_ref, sem):
    rows = source_ref.shape[1]
    per = out_ref.shape[1] // rows
    copies = []
    for e in range(slot_ref.shape[0]):
        dest = out_ref.at[e // per, pl.ds(e % per * rows, rows)]
        copies.append(pltpu.make_async_copy(source_ref.at[slot_ref[e]], dest, sem.at[e]))
        copies[-1].start()
    for copy in copies:
        copy.wait()


def pick_call(slots, source, spans):
    entries = slots.shape[0]
    _, rows, enc = source.shape
    return pl.pallas_call(
        pick_kernel,
        in_specs=[pl.BlockSpec(memory_space=pltpu.SMEM), pl.BlockSpec(memory_space=pl.ANY)],
        out_specs=pl.BlockSpec(memory_space=pltpu.VMEM),
        out_shape=jax.ShapeDtypeStruct((spans, entries // spans * rows, enc), BF16),
        scratch_shapes=[pltpu.SemaphoreType.DMA((entries,))],
        name="pick",
        cost_estimate=pl.CostEstimate(flops=0, bytes_accessed=3 * 10**6, transcendentals=0),
    )(slots, source)


NX = 4


def pairs_x(groups, shift):
    return [(d, d // NX * NX + (d % NX + shift) % NX) for d in range(groups)]


def pairs_z(groups, shift):
    return [(d, (d + shift * NX) % groups) for d in range(groups)]


def shards(queries, out_grad, key_weight, value_weight, encoded, nb_owner, nb_block):
    groups = lax.axis_size("dp")
    nz = groups // NX
    pipe = lax.axis_size("pipe")
    held, rows, enc = encoded.shape[1:]
    owners = nb_owner[0].reshape(-1)
    blocks = nb_block[0].reshape(-1)
    spans = nb_owner.shape[1]
    here, side = lax.axis_index("dp") // NX, lax.axis_index("dp") % NX
    over_x = [[z * NX + x for x in range(NX)] for z in range(nz)]

    def exchange(v, among=None):
        return lax.all_to_all(v, "dp", split_axis=0, concat_axis=0, tiled=True, axis_index_groups=among)

    weights = lax.all_gather(jnp.stack([key_weight[0], value_weight[0]])[None], "dp", axis=0, tiled=True)

    column_major = owners % NX * nz + owners // NX
    slot_ids = jnp.arange(groups, dtype=jnp.int32)[:, None]
    row_request = jnp.max(jnp.where(column_major[None, :] == slot_ids, blocks[None, :], -1), axis=1)
    row_wanted = exchange(row_request[:, None], over_x)[:, 0]

    def send_x(v, shift):
        return lax.ppermute(v, "dp", pairs_x(groups, shift))

    def send_z(v, shift):
        return lax.ppermute(v, "dp", pairs_z(groups, shift))

    own = encoded[0]
    ups, downs = [own], [own]
    for _ in range(nz // 2 - 1):
        ups.append(send_z(ups[-1], 1))
        downs.append(send_z(downs[-1], -1))
    half = held // 2
    far = jnp.concatenate([send_z(ups[-1][:half], 1), send_z(downs[-1][half:], -1)])
    table = jnp.concatenate([row_wanted, here[None]]).astype(jnp.int32)
    arrived = exchange(serve_call(table, ups + [far] + downs[:0:-1]), over_x)
    keys = pick_call(owners % NX * nz + (here - owners // NX) % nz, arrived, spans)
    incoming = lax.ppermute(out_grad, "pipe", [(s, (s - 1) % pipe) for s in range(pipe)])[0]

    request = jnp.max(jnp.where(owners[None, :] == slot_ids, blocks[None, :], -1), axis=1)
    wanted = exchange(request[:, None])[:, 0]

    by_side = jnp.take(row_wanted.reshape(NX, nz), (side - jnp.arange(NX)) % NX, axis=0)
    row_blocks = jnp.take(by_side, (here + jnp.arange(nz)) % nz, axis=1)
    keys, wanted, row_blocks = lax.optimization_barrier((keys, wanted, row_blocks))
    a, b, ds, p = scores_call(queries[0], incoming, weights, keys, 4)
    first = jnp.argmax(owners[:, None] == owners[None, :], axis=1).astype(jnp.int32)
    held_ids = jnp.arange(held, dtype=jnp.int32)

    hop_x, hop_z = (owners % NX - side) % NX, (owners // NX - here) % nz
    part = entry_call(hop_x * nz + hop_z, first, a, b, ds, p, groups, rows, 0, 2)
    pieces = [part[:nz]]
    for shift in range(1, NX):
        pieces.append(send_x(part[shift * nz : (shift + 1) * nz], shift))
    part = entry_call(owners, first, a, b, ds, p, groups, rows, 1, 2)
    returned = exchange(part)
    query_grad = query_call(ds, weights, keys, 4)

    row_sum = [jnp.zeros((nz, rows, enc // 2), F32)] * held
    for piece, asked in zip(pieces, row_blocks):
        for block in range(held):
            mine = (asked == block).astype(F32)[:, None, None]
            row_sum[block] = row_sum[block] + mine * piece.astype(F32)
    row_sum = jnp.stack(row_sum, axis=1).astype(BF16)
    left = row_sum[0].astype(F32)
    for shift in range(1, nz):
        left = left + send_z(row_sum[shift], shift).astype(F32)
    choose = (wanted[:, None] == held_ids[None, :]).astype(BF16)
    right = jnp.dot(choose.T, returned.reshape(groups, -1), preferred_element_type=F32)
    encoded_grad = jnp.concatenate([left, right.reshape(left.shape)], axis=-1)
    return query_grad[None], encoded_grad[None]


def solution(mesh):
    cut = P("pipe", "dp", None)
    deep = P("pipe", "dp", None, None)

    return jax.shard_map(
        shards,
        mesh=mesh,
        in_specs=(cut, cut, cut, cut, deep, cut, cut),
        out_specs=(cut, deep),
        check_vma=False,
    )
```

```python
import functools
import jax
import jax.numpy as jnp
from jax import lax
from jax.experimental import pallas as pl
from jax.experimental.pallas import tpu as pltpu
from jax.sharding import PartitionSpec as P

SPAN = 40
HEAD_DIM = 128
SCALE = HEAD_DIM ** (-0.5)
NX = 4
F32 = jnp.float32
BF16 = jnp.bfloat16


def dot(a, b, ca, cb):
    return lax.dot_general(a, b, (((ca,), (cb,)), ((), ())), preferred_element_type=F32)


def weight_copies(here, ring, dest, sems):
    nz = len(ring) - 1
    copies = []
    for i, piece in enumerate(ring):
        away = (i + 1) // 2 if i < nz else nz // 2
        away = away if i % 2 else nz - away
        row = here + nz - away
        row = jnp.where(row >= 2 * nz, row - 2 * nz, jnp.where(row >= nz, row - nz, row))
        count = piece.shape[0]
        start = row * NX + (NX - count if i == nz else 0)
        copies.append(pltpu.make_async_copy(piece, dest.at[pl.ds(start, count)], sems.at[i]))
    return copies


def key_copies(slot_ref, arrived, dest, sems):
    rows = arrived.shape[1]
    per = dest.shape[1] // rows
    return [
        pltpu.make_async_copy(
            arrived.at[slot_ref[e]], dest.at[e // per, pl.ds(e % per * rows, rows)], sems.at[e]
        )
        for e in range(slot_ref.shape[0])
    ]


def head_weight(block, h):
    ranks, _, width = block.shape
    per = width // HEAD_DIM
    rows = 16
    part = block[:, h // per * rows : (h // per + 1) * rows, h % per * HEAD_DIM : (h % per + 1) * HEAD_DIM]
    return part.reshape(ranks * rows, HEAD_DIM)


def grads_kernel(heads, pieces, slot_ref, here_ref, row_slot, dense_slot, first_ref, q_ref, g_ref, arrived, *refs):
    key_ring, value_ring = refs[:pieces], refs[pieces : 2 * pieces]
    ds_ref, row_ref, dense_ref = refs[2 * pieces : 2 * pieces + 3]
    key_w, value_w, keys_ref, a_ref, b_ref, sum_ref, sem_k, sem_v, sem_e = refs[2 * pieces + 3 :]
    step = pl.program_id(0)
    here = here_ref[0]
    of_keys = weight_copies(here, key_ring, key_w, sem_k)
    of_values = weight_copies(here, value_ring, value_w, sem_v)
    of_rows = key_copies(slot_ref, arrived, keys_ref, sem_e)

    @pl.when(step == 0)
    def _():
        for copy in of_keys + of_values + of_rows:
            copy.start()
        row_ref[...] = jnp.zeros_like(row_ref)
        dense_ref[...] = jnp.zeros_like(dense_ref)

    spans = a_ref.shape[0]
    rows = heads // (key_w.shape[2] // HEAD_DIM) * 16
    mine = pl.ds(pl.multiple_of(step * rows, rows), rows)
    for src, weight, out, copies in (
        (q_ref, key_w, a_ref, of_keys),
        (g_ref, value_w, b_ref, of_values),
    ):

        @pl.when(step == 0)
        def _():
            for copy in copies:
                copy.wait()

        block = weight[:, mine, :]
        for pair in range(heads // 2):
            wide = []
            for h in (2 * pair, 2 * pair + 1):
                wide.append(dot(src[:, h * HEAD_DIM : (h + 1) * HEAD_DIM], head_weight(block, h), 1, 1))
            for a in range(spans):
                part = slice(a * SPAN, (a + 1) * SPAN)
                both = jnp.concatenate([wide[0][part], wide[1][part]], axis=0)
                out[a, pair * 2 * SPAN : (pair + 1) * 2 * SPAN, :] = both.astype(BF16)

    @pl.when(step == 0)
    def _():
        for copy in of_rows:
            copy.wait()

    @pl.loop(0, spans)
    def _(a):
        keys = keys_ref[a]
        e = jnp.exp(SCALE * dot(keys, a_ref[a], 1, 1))
        total = jnp.sum(e, axis=0, keepdims=True)
        guard = jnp.where(total > 1e30, 2.0**-24, 1.0)
        probs = (e * guard) * (1.0 / (total * guard))
        grad = dot(keys, b_ref[a], 1, 1)
        delta = jnp.sum(probs * grad, axis=0, keepdims=True)
        ds = (probs * (grad - delta)).astype(BF16)
        ds_ref[a] = ds
        entry = SCALE * dot(ds, a_ref[a], 1, 0) + dot(probs.astype(BF16), b_ref[a], 1, 0)

        @pl.when(step == 0)
        def _():
            sum_ref[a] = entry

        @pl.when(step > 0)
        def _():
            sum_ref[a] = sum_ref[a] + entry

    @pl.when(step == pl.num_programs(0) - 1)
    def _():
        length = row_ref.shape[1]
        half = row_ref.shape[2]
        per = sum_ref.shape[1] // length
        for n in range(slot_ref.shape[0]):
            at = (n // per, slice(n % per * length, (n % per + 1) * length))
            first = first_ref[n]

            @pl.when(first != n)
            def _():
                span = first // per
                where = pl.ds(pl.multiple_of((first - span * per) * length, length), length)
                sum_ref[span, where] = sum_ref[span, where] + sum_ref[at]

        for n in range(slot_ref.shape[0]):
            at = (n // per, slice(n % per * length, (n % per + 1) * length))

            @pl.when(first_ref[n] == n)
            def _():
                value = sum_ref[at].astype(BF16)
                row_ref[row_slot[n]] = value[:, :half]
                dense_ref[dense_slot[n]] = value[:, half:]


def grads_call(slots, here, row_slot, dense_slot, first, q, g, arrived, key_ring, value_ring, spans, groups):
    tok, hd = q.shape
    ranks, rows, enc = arrived.shape
    entries = slots.shape[0]
    kr = entries // spans * rows
    heads = hd // HEAD_DIM // groups
    m = heads * SPAN
    cols = heads * HEAD_DIM
    pieces = len(key_ring)
    wide = (ranks,) + key_ring[0].shape[1:]
    anywhere = pl.BlockSpec(memory_space=pl.ANY)
    whole = pl.BlockSpec((ranks, rows, enc // 2), lambda i, *_: (0, 0, 0))
    return pl.pallas_call(
        functools.partial(grads_kernel, heads, pieces),
        grid_spec=pltpu.PrefetchScalarGridSpec(
            num_scalar_prefetch=5,
            grid=(groups,),
            in_specs=[
                pl.BlockSpec((tok, cols), lambda i, *_: (0, i)),
                pl.BlockSpec((tok, cols), lambda i, *_: (0, i)),
            ]
            + [anywhere] * (1 + 2 * pieces),
            out_specs=[pl.BlockSpec((spans, kr, m), lambda i, *_: (0, 0, i)), whole, whole],
            scratch_shapes=[
                pltpu.VMEM(wide, BF16),
                pltpu.VMEM(wide, BF16),
                pltpu.VMEM((spans, kr, enc), BF16),
                pltpu.VMEM((spans, m, enc), BF16),
                pltpu.VMEM((spans, m, enc), BF16),
                pltpu.VMEM((spans, kr, enc), F32),
                pltpu.SemaphoreType.DMA((pieces,)),
                pltpu.SemaphoreType.DMA((pieces,)),
                pltpu.SemaphoreType.DMA((entries,)),
            ],
        ),
        out_shape=[
            jax.ShapeDtypeStruct((spans, kr, m * groups), BF16),
            jax.ShapeDtypeStruct((ranks, rows, enc // 2), BF16),
            jax.ShapeDtypeStruct((ranks, rows, enc // 2), BF16),
        ],
        name="grads",
        cost_estimate=pl.CostEstimate(flops=10**10, bytes_accessed=25 * 10**6, transcendentals=2 * 10**6),
        compiler_params=pltpu.CompilerParams(vmem_limit_bytes=56 << 20),
    )(slots, here, row_slot, dense_slot, first, q, g, arrived, *key_ring, *value_ring)


def query_kernel(heads, pieces, slot_ref, here_ref, ds_ref, arrived, *refs):
    key_ring = refs[:pieces]
    o_ref, wide_ref, key_w, keys_ref, sem_k, sem_e = refs[pieces:]
    step = pl.program_id(0)

    @pl.when(step == 0)
    def _():
        copies = weight_copies(here_ref[0], key_ring, key_w, sem_k) + key_copies(
            slot_ref, arrived, keys_ref, sem_e
        )
        for copy in copies:
            copy.start()
        for copy in copies:
            copy.wait()

    spans = ds_ref.shape[0]
    rows = heads // (key_w.shape[2] // HEAD_DIM) * 16
    block = key_w[:, pl.ds(pl.multiple_of(step * rows, rows), rows), :]

    @pl.loop(0, spans)
    def _(a):
        wide = SCALE * dot(ds_ref[a], keys_ref[a], 0, 0)
        for h in range(heads):
            wide_ref[h, pl.ds(pl.multiple_of(a * SPAN, 8), SPAN), :] = wide[h * SPAN : (h + 1) * SPAN]

    for h in range(heads):
        cols = slice(h * HEAD_DIM, (h + 1) * HEAD_DIM)
        o_ref[:, cols] = dot(wide_ref[h].astype(BF16), head_weight(block, h), 1, 0).astype(BF16)


def query_call(slots, here, ds, arrived, key_ring, groups):
    spans, kr, m_all = ds.shape
    ranks, _, enc = arrived.shape
    entries = slots.shape[0]
    m = m_all // groups
    heads = m // SPAN
    cols = heads * HEAD_DIM
    tok = spans * SPAN
    pieces = len(key_ring)
    anywhere = pl.BlockSpec(memory_space=pl.ANY)
    return pl.pallas_call(
        functools.partial(query_kernel, heads, pieces),
        grid_spec=pltpu.PrefetchScalarGridSpec(
            num_scalar_prefetch=2,
            grid=(groups,),
            in_specs=[pl.BlockSpec((spans, kr, m), lambda i, *_: (0, 0, i))] + [anywhere] * (1 + pieces),
            out_specs=pl.BlockSpec((tok, cols), lambda i, *_: (0, i)),
            scratch_shapes=[
                pltpu.VMEM((heads, tok, enc), F32),
                pltpu.VMEM((ranks,) + key_ring[0].shape[1:], BF16),
                pltpu.VMEM((spans, kr, enc), BF16),
                pltpu.SemaphoreType.DMA((pieces,)),
                pltpu.SemaphoreType.DMA((entries,)),
            ],
        ),
        out_shape=jax.ShapeDtypeStruct((tok, cols * groups), BF16),
        name="query_grad",
        cost_estimate=pl.CostEstimate(flops=3 * 10**9, bytes_accessed=12 * 10**6, transcendentals=0),
        compiler_params=pltpu.CompilerParams(vmem_limit_bytes=56 << 20),
    )(slots, here, ds, arrived, *key_ring)


def serve_kernel(table_ref, *refs):
    sources, (out_ref, sem) = refs[:-2], refs[-2:]
    steps = len(sources)
    here = table_ref[out_ref.shape[0]]
    copies = []
    for slot in range(out_ref.shape[0]):
        back = slot % steps
        row = jnp.where(here >= back, here - back, here - back + steps)
        block = jnp.maximum(table_ref[slot // steps * steps + row], 0)
        copies.append(pltpu.make_async_copy(sources[back].at[block], out_ref.at[slot], sem.at[slot]))
        copies[-1].start()
    for copy in copies:
        copy.wait()


def serve_call(table, sources):
    _, rows, enc = sources[0].shape
    slots = table.shape[0] - 1
    return pl.pallas_call(
        serve_kernel,
        in_specs=[pl.BlockSpec(memory_space=pltpu.SMEM)]
        + [pl.BlockSpec(memory_space=pl.ANY)] * len(sources),
        out_specs=pl.BlockSpec(memory_space=pltpu.VMEM),
        out_shape=jax.ShapeDtypeStruct((slots, rows, enc), BF16),
        scratch_shapes=[pltpu.SemaphoreType.DMA((slots,))],
        name="serve",
        cost_estimate=pl.CostEstimate(flops=0, bytes_accessed=8 * 10**6, transcendentals=0),
    )(table, *sources)


def pairs_x(groups, shift):
    return [(d, d // NX * NX + (d % NX + shift) % NX) for d in range(groups)]


def pairs_z(groups, shift):
    return [(d, (d + shift * NX) % groups) for d in range(groups)]


def tied(value, *others):
    return lax.optimization_barrier((value,) + others)[0]


def shards(queries, out_grad, key_weight, value_weight, encoded, nb_owner, nb_block):
    groups = lax.axis_size("dp")
    nz = groups // NX
    pipe = lax.axis_size("pipe")
    held, rows, enc = encoded.shape[1:]
    owners = nb_owner[0].reshape(-1)
    blocks = nb_block[0].reshape(-1)
    spans = nb_owner.shape[1]
    here, side = lax.axis_index("dp") // NX, lax.axis_index("dp") % NX
    over_x = [[z * NX + x for x in range(NX)] for z in range(nz)]

    def exchange(v, among=None):
        return lax.all_to_all(v, "dp", split_axis=0, concat_axis=0, tiled=True, axis_index_groups=among)

    def send_x(v, shift):
        return lax.ppermute(v, "dp", pairs_x(groups, shift))

    def send_z(v, shift):
        return lax.ppermute(v, "dp", pairs_z(groups, shift))

    def ring_move(ring):
        up, down = ring[-2:] if len(ring) > 1 else ring * 2
        if len(ring) == nz - 1:
            half = up.shape[0] // 2
            up, down = up[:half], down[half:]
        return ring + [send_z(up, 1), send_z(down, -1)]

    def pieces_of(weight):
        _, rows, _ = weight.shape
        cols = 4 * HEAD_DIM
        return weight.reshape(rows, -1, cols).swapaxes(0, 1).reshape(-1, cols)

    mine = jnp.stack([pieces_of(key_weight), pieces_of(value_weight)])
    row_weights = exchange(jnp.broadcast_to(mine[None], (NX,) + mine.shape), over_x)
    held_rows = ring_move([encoded[0]])
    held_rows[1:] = lax.optimization_barrier((held_rows[1], held_rows[2], row_weights))[:2]

    column_major = owners % NX * nz + owners // NX
    slot_ids = jnp.arange(groups, dtype=jnp.int32)[:, None]
    request = jnp.max(jnp.where(column_major[None, :] == slot_ids, blocks[None, :], -1), axis=1)
    by_column = jnp.broadcast_to(request.reshape(1, NX, nz), (nz, NX, nz)).reshape(groups, nz)
    asked = exchange(tied(by_column, row_weights))
    wanted = lax.dynamic_slice_in_dim(asked, here, 1, axis=1)[:, 0]
    row_wanted = lax.dynamic_slice_in_dim(asked, here * NX, NX, axis=0)

    keys, values = [row_weights[:, 0]], [row_weights[:, 1]]
    for _ in range(nz // 2 - 1):
        held_rows = ring_move(held_rows)
    for _ in range(nz // 2):
        keys, values = ring_move(keys), ring_move(values)
    far = jnp.concatenate(held_rows[-2:])
    in_order = held_rows[:1] + held_rows[1 : nz - 1 : 2] + [far] + held_rows[nz - 2 : 0 : -2]
    table = jnp.concatenate([row_wanted.reshape(-1), here[None]]).astype(jnp.int32)
    served = serve_call(table, in_order)
    arrived = exchange(served, over_x)
    incoming = lax.ppermute(out_grad, "pipe", [(s, (s - 1) % pipe) for s in range(pipe)])[0]

    slots = (owners % NX * nz + (here - owners // NX) % nz).astype(jnp.int32)
    hop_x, hop_z = (owners % NX - side) % NX, (owners // NX - here) % nz
    row_slot = (hop_x * nz + hop_z).astype(jnp.int32)
    first = jnp.argmax(owners[:, None] == owners[None, :], axis=1).astype(jnp.int32)
    by_side = jnp.take(row_wanted, (side - jnp.arange(NX)) % NX, axis=0)
    row_blocks = jnp.take(by_side, (here + jnp.arange(nz)) % nz, axis=1)
    at = here[None].astype(jnp.int32)
    slots, first, row_slot, wanted, row_blocks = lax.optimization_barrier(
        (slots, first, row_slot, wanted, row_blocks)
    )

    ds, part, dense = grads_call(
        slots, at, row_slot, owners, first, queries[0], incoming, arrived, keys, values, spans, 2
    )
    returned = exchange(dense)
    pieces = [part[:nz]]
    for shift in range(1, NX):
        pieces.append(send_x(part[shift * nz : (shift + 1) * nz], shift))
    query_grad = query_call(slots, at, ds, arrived, keys, 2)

    held_ids = jnp.arange(held, dtype=jnp.int32)
    row_sum = [jnp.zeros((nz, rows, enc // 2), F32)] * held
    for piece, of_piece in zip(pieces, row_blocks):
        for block in range(held):
            chosen = (of_piece == block).astype(F32)[:, None, None]
            row_sum[block] = row_sum[block] + chosen * piece.astype(F32)
    row_sum = jnp.stack(row_sum, axis=1).astype(BF16)
    left = row_sum[0].astype(F32)
    for shift in range(1, nz):
        left = left + send_z(row_sum[shift], shift).astype(F32)
    choose = (wanted[:, None] == held_ids[None, :]).astype(BF16)
    right = jnp.dot(choose.T, returned.reshape(groups, -1), preferred_element_type=F32)
    encoded_grad = jnp.concatenate([left, right.reshape(left.shape)], axis=-1)
    return query_grad[None], encoded_grad[None]


def solution(mesh):
    cut = P("pipe", "dp", None)
    deep = P("pipe", "dp", None, None)

    return jax.shard_map(
        shards,
        mesh=mesh,
        in_specs=(cut, cut, cut, cut, deep, cut, cut),
        out_specs=(cut, deep),
        check_vma=False,
    )
```

```python
import functools
import jax
import jax.numpy as jnp
from jax import lax
from jax.experimental import pallas as pl
from jax.experimental.pallas import tpu as pltpu
from jax.sharding import PartitionSpec as P

SPAN = 40
HEAD_DIM = 128
SCALE = HEAD_DIM ** (-0.5)
NX = 4
F32 = jnp.float32
BF16 = jnp.bfloat16


def dot(a, b, ca, cb):
    return lax.dot_general(a, b, (((ca,), (cb,)), ((), ())), preferred_element_type=F32)


def weight_copies(here, ring, dest, sems):
    nz = len(ring) - 1
    copies = []
    for i, piece in enumerate(ring):
        away = (i + 1) // 2 if i < nz else nz // 2
        away = away if i % 2 else nz - away
        row = here + nz - away
        row = jnp.where(row >= 2 * nz, row - 2 * nz, jnp.where(row >= nz, row - nz, row))
        count = piece.shape[0]
        start = row * NX + (NX - count if i == nz else 0)
        copies.append(pltpu.make_async_copy(piece, dest.at[pl.ds(start, count)], sems.at[i]))
    return copies


def key_copies(slot_ref, arrived, dest, sems):
    rows = arrived.shape[1]
    per = dest.shape[1] // rows
    return [
        pltpu.make_async_copy(
            arrived.at[slot_ref[e]], dest.at[e // per, pl.ds(e % per * rows, rows)], sems.at[e]
        )
        for e in range(slot_ref.shape[0])
    ]


def head_weight(block, h):
    ranks, _, width = block.shape
    per = width // HEAD_DIM
    rows = 16
    part = block[:, h // per * rows : (h // per + 1) * rows, h % per * HEAD_DIM : (h % per + 1) * HEAD_DIM]
    return part.reshape(ranks * rows, HEAD_DIM)


def grads_kernel(heads, pieces, slot_ref, here_ref, row_slot, dense_slot, first_ref, q_ref, g_ref, arrived, *refs):
    key_ring, value_ring = refs[:pieces], refs[pieces : 2 * pieces]
    ds_ref, row_ref, dense_ref = refs[2 * pieces : 2 * pieces + 3]
    key_w, value_w, keys_ref, a_ref, b_ref, sum_ref, sem_k, sem_v, sem_e = refs[2 * pieces + 3 :]
    step = pl.program_id(0)
    here = here_ref[0]
    of_keys = weight_copies(here, key_ring, key_w, sem_k)
    of_values = weight_copies(here, value_ring, value_w, sem_v)
    of_rows = key_copies(slot_ref, arrived, keys_ref, sem_e)

    @pl.when(step == 0)
    def _():
        for copy in of_keys + of_values + of_rows:
            copy.start()

        @pl.loop(0, row_ref.shape[0])
        def _(n):
            row_ref[n] = jnp.zeros(row_ref.shape[1:], BF16)
            dense_ref[n] = jnp.zeros(row_ref.shape[1:], BF16)

    spans = a_ref.shape[0]
    quad = key_w.shape[2] // HEAD_DIM
    for src, weight, out, copies in (
        (q_ref, key_w, a_ref, of_keys),
        (g_ref, value_w, b_ref, of_values),
    ):

        @pl.when(step == 0)
        def _():
            for copy in copies:
                copy.wait()

        @pl.loop(0, heads // quad)
        def _(q):
            block = weight[:, pl.ds(pl.multiple_of((step * (heads // quad) + q) * 16, 16), 16), :]
            source = src[:, pl.ds(pl.multiple_of(q * quad * HEAD_DIM, quad * HEAD_DIM), quad * HEAD_DIM)]
            for pair in range(quad // 2):
                wide = []
                for h in (2 * pair, 2 * pair + 1):
                    wide.append(dot(source[:, h * HEAD_DIM : (h + 1) * HEAD_DIM], head_weight(block, h), 1, 1))
                rows = pl.ds(pl.multiple_of((q * quad + 2 * pair) * SPAN, 16), 2 * SPAN)
                for a in range(spans):
                    part = slice(a * SPAN, (a + 1) * SPAN)
                    both = jnp.concatenate([wide[0][part], wide[1][part]], axis=0)
                    out[a, rows, :] = both.astype(BF16)

    @pl.when(step == 0)
    def _():
        for copy in of_rows:
            copy.wait()

    @pl.loop(0, spans)
    def _(a):
        keys = keys_ref[a]
        e = jnp.exp(SCALE * dot(keys, a_ref[a], 1, 1))
        total = jnp.sum(e, axis=0, keepdims=True)
        guard = jnp.where(total > 1e30, 2.0**-24, 1.0)
        probs = (e * guard) * (1.0 / (total * guard))
        grad = dot(keys, b_ref[a], 1, 1)
        delta = jnp.sum(probs * grad, axis=0, keepdims=True)
        ds = (probs * (grad - delta)).astype(BF16)
        ds_ref[a] = ds
        entry = SCALE * dot(ds, a_ref[a], 1, 0) + dot(probs.astype(BF16), b_ref[a], 1, 0)

        @pl.when(step == 0)
        def _():
            sum_ref[a] = entry

        @pl.when(step > 0)
        def _():
            sum_ref[a] = sum_ref[a] + entry

    @pl.when(step == pl.num_programs(0) - 1)
    def _():
        length = row_ref.shape[1]
        half = row_ref.shape[2]
        per = sum_ref.shape[1] // length

        def rows_of(n):
            span = n // per
            return span, pl.ds(pl.multiple_of((n - span * per) * length, length), length)

        @pl.loop(0, slot_ref.shape[0])
        def _(n):
            first = first_ref[n]

            @pl.when(first != n)
            def _():
                sum_ref[rows_of(first)] = sum_ref[rows_of(first)] + sum_ref[rows_of(n)]

        @pl.loop(0, slot_ref.shape[0])
        def _(n):
            @pl.when(first_ref[n] == n)
            def _():
                value = sum_ref[rows_of(n)].astype(BF16)
                row_ref[row_slot[n]] = value[:, :half]
                dense_ref[dense_slot[n]] = value[:, half:]


def grads_call(slots, here, row_slot, dense_slot, first, q, g, arrived, key_ring, value_ring, spans, groups):
    tok, hd = q.shape
    ranks, rows, enc = arrived.shape
    entries = slots.shape[0]
    kr = entries // spans * rows
    heads = hd // HEAD_DIM // groups
    m = heads * SPAN
    cols = heads * HEAD_DIM
    pieces = len(key_ring)
    wide = (ranks,) + key_ring[0].shape[1:]
    anywhere = pl.BlockSpec(memory_space=pl.ANY)
    whole = pl.BlockSpec((ranks, rows, enc // 2), lambda i, *_: (0, 0, 0))
    return pl.pallas_call(
        functools.partial(grads_kernel, heads, pieces),
        grid_spec=pltpu.PrefetchScalarGridSpec(
            num_scalar_prefetch=5,
            grid=(groups,),
            in_specs=[
                pl.BlockSpec((tok, cols), lambda i, *_: (0, i)),
                pl.BlockSpec((tok, cols), lambda i, *_: (0, i)),
            ]
            + [anywhere] * (1 + 2 * pieces),
            out_specs=[pl.BlockSpec((spans, kr, m), lambda i, *_: (0, 0, i)), whole, whole],
            scratch_shapes=[
                pltpu.VMEM(wide, BF16),
                pltpu.VMEM(wide, BF16),
                pltpu.VMEM((spans, kr, enc), BF16),
                pltpu.VMEM((spans, m, enc), BF16),
                pltpu.VMEM((spans, m, enc), BF16),
                pltpu.VMEM((spans, kr, enc), F32),
                pltpu.SemaphoreType.DMA((pieces,)),
                pltpu.SemaphoreType.DMA((pieces,)),
                pltpu.SemaphoreType.DMA((entries,)),
            ],
        ),
        out_shape=[
            jax.ShapeDtypeStruct((spans, kr, m * groups), BF16),
            jax.ShapeDtypeStruct((ranks, rows, enc // 2), BF16),
            jax.ShapeDtypeStruct((ranks, rows, enc // 2), BF16),
        ],
        name="grads",
        cost_estimate=pl.CostEstimate(flops=10**10, bytes_accessed=25 * 10**6, transcendentals=2 * 10**6),
        compiler_params=pltpu.CompilerParams(vmem_limit_bytes=56 << 20),
    )(slots, here, row_slot, dense_slot, first, q, g, arrived, *key_ring, *value_ring)


def query_kernel(heads, pieces, slot_ref, here_ref, ds_ref, arrived, *refs):
    key_ring = refs[:pieces]
    o_ref, wide_ref, key_w, keys_ref, sem_k, sem_e = refs[pieces:]
    step = pl.program_id(0)

    @pl.when(step == 0)
    def _():
        copies = weight_copies(here_ref[0], key_ring, key_w, sem_k) + key_copies(
            slot_ref, arrived, keys_ref, sem_e
        )
        for copy in copies:
            copy.start()
        for copy in copies:
            copy.wait()

    spans = ds_ref.shape[0]
    quad = key_w.shape[2] // HEAD_DIM

    @pl.loop(0, spans)
    def _(a):
        wide = SCALE * dot(ds_ref[a], keys_ref[a], 0, 0)
        for h in range(heads):
            wide_ref[h, pl.ds(pl.multiple_of(a * SPAN, 8), SPAN), :] = wide[h * SPAN : (h + 1) * SPAN]

    @pl.loop(0, heads // quad)
    def _(q):
        block = key_w[:, pl.ds(pl.multiple_of((step * (heads // quad) + q) * 16, 16), 16), :]
        parts = [
            dot(wide_ref[q * quad + h].astype(BF16), head_weight(block, h), 1, 0).astype(BF16)
            for h in range(quad)
        ]
        width = quad * HEAD_DIM
        o_ref[:, pl.ds(pl.multiple_of(q * width, width), width)] = jnp.concatenate(parts, axis=1)


def query_call(slots, here, ds, arrived, key_ring, groups):
    spans, kr, m_all = ds.shape
    ranks, _, enc = arrived.shape
    entries = slots.shape[0]
    m = m_all // groups
    heads = m // SPAN
    cols = heads * HEAD_DIM
    tok = spans * SPAN
    pieces = len(key_ring)
    anywhere = pl.BlockSpec(memory_space=pl.ANY)
    return pl.pallas_call(
        functools.partial(query_kernel, heads, pieces),
        grid_spec=pltpu.PrefetchScalarGridSpec(
            num_scalar_prefetch=2,
            grid=(groups,),
            in_specs=[pl.BlockSpec((spans, kr, m), lambda i, *_: (0, 0, i))] + [anywhere] * (1 + pieces),
            out_specs=pl.BlockSpec((tok, cols), lambda i, *_: (0, i)),
            scratch_shapes=[
                pltpu.VMEM((heads, tok, enc), F32),
                pltpu.VMEM((ranks,) + key_ring[0].shape[1:], BF16),
                pltpu.VMEM((spans, kr, enc), BF16),
                pltpu.SemaphoreType.DMA((pieces,)),
                pltpu.SemaphoreType.DMA((entries,)),
            ],
        ),
        out_shape=jax.ShapeDtypeStruct((tok, cols * groups), BF16),
        name="query_grad",
        cost_estimate=pl.CostEstimate(flops=3 * 10**9, bytes_accessed=12 * 10**6, transcendentals=0),
        compiler_params=pltpu.CompilerParams(vmem_limit_bytes=56 << 20),
    )(slots, here, ds, arrived, *key_ring)


def serve_kernel(table_ref, *refs):
    sources, (out_ref, sem) = refs[:-2], refs[-2:]
    steps = len(sources)
    here = table_ref[out_ref.shape[0]]
    copies = []
    for slot in range(out_ref.shape[0]):
        back = slot % steps
        row = jnp.where(here >= back, here - back, here - back + steps)
        block = jnp.maximum(table_ref[slot // steps * steps + row], 0)
        copies.append(pltpu.make_async_copy(sources[back].at[block], out_ref.at[slot], sem.at[slot]))
        copies[-1].start()
    for copy in copies:
        copy.wait()


def serve_call(table, sources):
    _, rows, enc = sources[0].shape
    slots = table.shape[0] - 1
    return pl.pallas_call(
        serve_kernel,
        in_specs=[pl.BlockSpec(memory_space=pltpu.SMEM)]
        + [pl.BlockSpec(memory_space=pl.ANY)] * len(sources),
        out_specs=pl.BlockSpec(memory_space=pltpu.VMEM),
        out_shape=jax.ShapeDtypeStruct((slots, rows, enc), BF16),
        scratch_shapes=[pltpu.SemaphoreType.DMA((slots,))],
        name="serve",
        cost_estimate=pl.CostEstimate(flops=0, bytes_accessed=8 * 10**6, transcendentals=0),
    )(table, *sources)


def pairs_x(groups, shift):
    return [(d, d // NX * NX + (d % NX + shift) % NX) for d in range(groups)]


def pairs_z(groups, shift):
    return [(d, (d + shift * NX) % groups) for d in range(groups)]


def tied(value, *others):
    return lax.optimization_barrier((value,) + others)[0]


def shards(queries, out_grad, key_weight, value_weight, encoded, nb_owner, nb_block):
    groups = lax.axis_size("dp")
    nz = groups // NX
    pipe = lax.axis_size("pipe")
    held, rows, enc = encoded.shape[1:]
    owners = nb_owner[0].reshape(-1)
    blocks = nb_block[0].reshape(-1)
    spans = nb_owner.shape[1]
    here, side = lax.axis_index("dp") // NX, lax.axis_index("dp") % NX
    over_x = [[z * NX + x for x in range(NX)] for z in range(nz)]

    def exchange(v, among=None):
        return lax.all_to_all(v, "dp", split_axis=0, concat_axis=0, tiled=True, axis_index_groups=among)

    def send_x(v, shift):
        return lax.ppermute(v, "dp", pairs_x(groups, shift))

    def send_z(v, shift):
        return lax.ppermute(v, "dp", pairs_z(groups, shift))

    def ring_move(ring):
        up, down = ring[-2:] if len(ring) > 1 else ring * 2
        if len(ring) == nz - 1:
            half = up.shape[0] // 2
            up, down = up[:half], down[half:]
        return ring + [send_z(up, 1), send_z(down, -1)]

    def pieces_of(weight):
        _, rows, _ = weight.shape
        cols = 4 * HEAD_DIM
        return weight.reshape(rows, -1, cols).swapaxes(0, 1).reshape(-1, cols)

    mine = jnp.stack([pieces_of(key_weight), pieces_of(value_weight)])
    row_weights = exchange(jnp.broadcast_to(mine[None], (NX,) + mine.shape), over_x)
    held_rows = ring_move([encoded[0]])
    held_rows[1:] = lax.optimization_barrier((held_rows[1], held_rows[2], row_weights))[:2]

    column_major = owners % NX * nz + owners // NX
    slot_ids = jnp.arange(groups, dtype=jnp.int32)[:, None]
    request = jnp.max(jnp.where(column_major[None, :] == slot_ids, blocks[None, :], -1), axis=1)
    by_column = jnp.broadcast_to(request.reshape(1, NX, nz), (nz, NX, nz)).reshape(groups, nz)
    asked = exchange(tied(by_column, row_weights))
    wanted = lax.dynamic_slice_in_dim(asked, here, 1, axis=1)[:, 0]
    row_wanted = lax.dynamic_slice_in_dim(asked, here * NX, NX, axis=0)

    keys, values = [row_weights[:, 0]], [row_weights[:, 1]]
    for _ in range(nz // 2 - 1):
        held_rows = ring_move(held_rows)
    for _ in range(nz // 2):
        keys, values = ring_move(keys), ring_move(values)
    far = jnp.concatenate(held_rows[-2:])
    in_order = held_rows[:1] + held_rows[1 : nz - 1 : 2] + [far] + held_rows[nz - 2 : 0 : -2]
    table = jnp.concatenate([row_wanted.reshape(-1), here[None]]).astype(jnp.int32)
    served = serve_call(table, in_order)
    arrived = exchange(served, over_x)
    incoming = lax.ppermute(out_grad, "pipe", [(s, (s - 1) % pipe) for s in range(pipe)])[0]

    slots = (owners % NX * nz + (here - owners // NX) % nz).astype(jnp.int32)
    hop_x, hop_z = (owners % NX - side) % NX, (owners // NX - here) % nz
    row_slot = (hop_x * nz + hop_z).astype(jnp.int32)
    first = jnp.argmax(owners[:, None] == owners[None, :], axis=1).astype(jnp.int32)
    by_side = jnp.take(row_wanted, (side - jnp.arange(NX)) % NX, axis=0)
    row_blocks = jnp.take(by_side, (here + jnp.arange(nz)) % nz, axis=1)
    at = here[None].astype(jnp.int32)
    slots, first, row_slot, wanted, row_blocks = lax.optimization_barrier(
        (slots, first, row_slot, wanted, row_blocks)
    )

    ds, part, dense = grads_call(
        slots, at, row_slot, owners, first, queries[0], incoming, arrived, keys, values, spans, 2
    )
    returned = exchange(dense)
    pieces = [part[:nz]]
    for shift in range(1, NX):
        pieces.append(send_x(part[shift * nz : (shift + 1) * nz], shift))
    query_grad = query_call(slots, at, ds, arrived, keys, 2)

    held_ids = jnp.arange(held, dtype=jnp.int32)
    row_sum = [jnp.zeros((nz, rows, enc // 2), F32)] * held
    for piece, of_piece in zip(pieces, row_blocks):
        for block in range(held):
            chosen = (of_piece == block).astype(F32)[:, None, None]
            row_sum[block] = row_sum[block] + chosen * piece.astype(F32)
    row_sum = jnp.stack(row_sum, axis=1).astype(BF16)
    left = row_sum[0].astype(F32)
    for shift in range(1, nz):
        left = left + send_z(row_sum[shift], shift).astype(F32)
    choose = (wanted[:, None] == held_ids[None, :]).astype(BF16)
    right = jnp.dot(choose.T, returned.reshape(groups, -1), preferred_element_type=F32)
    encoded_grad = jnp.concatenate([left, right.reshape(left.shape)], axis=-1)
    return query_grad[None], encoded_grad[None]


def solution(mesh):
    cut = P("pipe", "dp", None)
    deep = P("pipe", "dp", None, None)

    return jax.shard_map(
        shards,
        mesh=mesh,
        in_specs=(cut, cut, cut, cut, deep, cut, cut),
        out_specs=(cut, deep),
        check_vma=False,
    )
```

```python
import functools
import jax
import jax.numpy as jnp
from jax import lax
from jax.experimental import pallas as pl
from jax.experimental.pallas import tpu as pltpu
from jax.sharding import PartitionSpec as P

SPAN = 40
HEAD_DIM = 128
SCALE = HEAD_DIM ** (-0.5)
NX = 4
F32 = jnp.float32
BF16 = jnp.bfloat16


def dot(a, b, ca, cb):
    return lax.dot_general(a, b, (((ca,), (cb,)), ((), ())), preferred_element_type=F32)


def weight_copies(here, ring, dest, sems):
    nz = len(ring) - 1
    copies = []
    for i, piece in enumerate(ring):
        away = (i + 1) // 2 if i < nz else nz // 2
        away = away if i % 2 else nz - away
        row = here + nz - away
        row = jnp.where(row >= 2 * nz, row - 2 * nz, jnp.where(row >= nz, row - nz, row))
        count = piece.shape[0]
        start = row * NX + (NX - count if i == nz else 0)
        copies.append(pltpu.make_async_copy(piece, dest.at[pl.ds(start, count)], sems.at[i]))
    return copies


def key_copies(slot_ref, arrived, dest, sems):
    rows = arrived.shape[1]
    per = dest.shape[1] // rows
    return [
        pltpu.make_async_copy(
            arrived.at[slot_ref[e]], dest.at[e // per, pl.ds(e % per * rows, rows)], sems.at[e]
        )
        for e in range(slot_ref.shape[0])
    ]


def head_weight(block, h):
    ranks, _, width = block.shape
    per = width // HEAD_DIM
    rows = 16
    part = block[:, h // per * rows : (h // per + 1) * rows, h % per * HEAD_DIM : (h % per + 1) * HEAD_DIM]
    return part.reshape(ranks * rows, HEAD_DIM)


def grads_kernel(heads, pieces, slot_ref, here_ref, row_slot, dense_slot, first_ref, q_ref, g_ref, arrived, *refs):
    key_ring, value_ring = refs[:pieces], refs[pieces : 2 * pieces]
    ds_ref, dense_ref = refs[2 * pieces : 2 * pieces + 2]
    row_refs = refs[2 * pieces + 2 : 2 * pieces + 2 + NX]
    key_w, value_w, keys_ref, a_ref, b_ref, sum_ref, sem_k, sem_v, sem_e = refs[2 * pieces + 2 + NX :]
    step = pl.program_id(0)
    here = here_ref[0]
    of_keys = weight_copies(here, key_ring, key_w, sem_k)
    of_values = weight_copies(here, value_ring, value_w, sem_v)
    of_rows = key_copies(slot_ref, arrived, keys_ref, sem_e)

    @pl.when(step == 0)
    def _():
        for copy in of_keys + of_values + of_rows:
            copy.start()

        blank = jnp.zeros(dense_ref.shape[1:], BF16)

        @pl.loop(0, row_refs[0].shape[0])
        def _(n):
            for x, row_ref in enumerate(row_refs):
                row_ref[n] = blank
                dense_ref[n * NX + x] = blank

    spans = a_ref.shape[0]
    quad = key_w.shape[2] // HEAD_DIM
    for src, weight, out, copies in (
        (q_ref, key_w, a_ref, of_keys),
        (g_ref, value_w, b_ref, of_values),
    ):

        @pl.when(step == 0)
        def _():
            for copy in copies:
                copy.wait()

        @pl.loop(0, heads // quad)
        def _(q):
            block = weight[:, pl.ds(pl.multiple_of((step * (heads // quad) + q) * 16, 16), 16), :]
            source = src[:, pl.ds(pl.multiple_of(q * quad * HEAD_DIM, quad * HEAD_DIM), quad * HEAD_DIM)]
            for pair in range(quad // 2):
                wide = []
                for h in (2 * pair, 2 * pair + 1):
                    wide.append(dot(source[:, h * HEAD_DIM : (h + 1) * HEAD_DIM], head_weight(block, h), 1, 1))
                rows = pl.ds(pl.multiple_of((q * quad + 2 * pair) * SPAN, 16), 2 * SPAN)
                for a in range(spans):
                    part = slice(a * SPAN, (a + 1) * SPAN)
                    both = jnp.concatenate([wide[0][part], wide[1][part]], axis=0)
                    out[a, rows, :] = both.astype(BF16)

    @pl.when(step == 0)
    def _():
        for copy in of_rows:
            copy.wait()

    @pl.loop(0, spans)
    def _(a):
        keys = keys_ref[a]
        e = jnp.exp(SCALE * dot(keys, a_ref[a], 1, 1))
        total = jnp.sum(e, axis=0, keepdims=True)
        guard = jnp.where(total > 1e30, 2.0**-24, 1.0)
        probs = (e * guard) * (1.0 / (total * guard))
        grad = dot(keys, b_ref[a], 1, 1)
        delta = jnp.sum(probs * grad, axis=0, keepdims=True)
        ds = (probs * (grad - delta)).astype(BF16)
        ds_ref[a] = ds
        entry = SCALE * dot(ds, a_ref[a], 1, 0) + dot(probs.astype(BF16), b_ref[a], 1, 0)

        @pl.when(step == 0)
        def _():
            sum_ref[a] = entry

        @pl.when(step > 0)
        def _():
            sum_ref[a] = sum_ref[a] + entry

    @pl.when(step == pl.num_programs(0) - 1)
    def _():
        length = dense_ref.shape[1]
        half = dense_ref.shape[2]
        nz = row_refs[0].shape[0]
        per = sum_ref.shape[1] // length

        def rows_of(n):
            span = n // per
            return span, pl.ds(pl.multiple_of((n - span * per) * length, length), length)

        @pl.loop(0, slot_ref.shape[0])
        def _(n):
            first = first_ref[n]

            @pl.when(first != n)
            def _():
                sum_ref[rows_of(first)] = sum_ref[rows_of(first)] + sum_ref[rows_of(n)]

        @pl.loop(0, slot_ref.shape[0])
        def _(n):
            @pl.when(first_ref[n] == n)
            def _():
                value = sum_ref[rows_of(n)].astype(BF16)
                for x, row_ref in enumerate(row_refs):
                    at = row_slot[n] - x * nz

                    @pl.when((at >= 0) & (at < nz))
                    def _():
                        row_ref[at] = value[:, :half]

                dense_ref[dense_slot[n]] = value[:, half:]


def grads_call(slots, here, row_slot, dense_slot, first, q, g, arrived, key_ring, value_ring, spans, groups):
    tok, hd = q.shape
    ranks, rows, enc = arrived.shape
    entries = slots.shape[0]
    kr = entries // spans * rows
    heads = hd // HEAD_DIM // groups
    m = heads * SPAN
    cols = heads * HEAD_DIM
    pieces = len(key_ring)
    wide = (ranks,) + key_ring[0].shape[1:]
    anywhere = pl.BlockSpec(memory_space=pl.ANY)
    whole = pl.BlockSpec((ranks, rows, enc // 2), lambda i, *_: (0, 0, 0))
    piece = pl.BlockSpec((ranks // NX, rows, enc // 2), lambda i, *_: (0, 0, 0))
    return pl.pallas_call(
        functools.partial(grads_kernel, heads, pieces),
        grid_spec=pltpu.PrefetchScalarGridSpec(
            num_scalar_prefetch=5,
            grid=(groups,),
            in_specs=[
                pl.BlockSpec((tok, cols), lambda i, *_: (0, i)),
                pl.BlockSpec((tok, cols), lambda i, *_: (0, i)),
            ]
            + [anywhere] * (1 + 2 * pieces),
            out_specs=[pl.BlockSpec((spans, kr, m), lambda i, *_: (0, 0, i)), whole] + [piece] * NX,
            scratch_shapes=[
                pltpu.VMEM(wide, BF16),
                pltpu.VMEM(wide, BF16),
                pltpu.VMEM((spans, kr, enc), BF16),
                pltpu.VMEM((spans, m, enc), BF16),
                pltpu.VMEM((spans, m, enc), BF16),
                pltpu.VMEM((spans, kr, enc), F32),
                pltpu.SemaphoreType.DMA((pieces,)),
                pltpu.SemaphoreType.DMA((pieces,)),
                pltpu.SemaphoreType.DMA((entries,)),
            ],
        ),
        out_shape=[
            jax.ShapeDtypeStruct((spans, kr, m * groups), BF16),
            jax.ShapeDtypeStruct((ranks, rows, enc // 2), BF16),
        ]
        + [jax.ShapeDtypeStruct((ranks // NX, rows, enc // 2), BF16)] * NX,
        name="grads",
        cost_estimate=pl.CostEstimate(flops=10**10, bytes_accessed=25 * 10**6, transcendentals=2 * 10**6),
        compiler_params=pltpu.CompilerParams(vmem_limit_bytes=60 << 20),
    )(slots, here, row_slot, dense_slot, first, q, g, arrived, *key_ring, *value_ring)


def query_kernel(heads, pieces, slot_ref, here_ref, ds_ref, arrived, *refs):
    key_ring = refs[:pieces]
    o_ref, wide_ref, key_w, keys_ref, sem_k, sem_e = refs[pieces:]
    step = pl.program_id(0)

    @pl.when(step == 0)
    def _():
        copies = weight_copies(here_ref[0], key_ring, key_w, sem_k) + key_copies(
            slot_ref, arrived, keys_ref, sem_e
        )
        for copy in copies:
            copy.start()
        for copy in copies:
            copy.wait()

    spans = ds_ref.shape[0]
    quad = key_w.shape[2] // HEAD_DIM

    @pl.loop(0, spans)
    def _(a):
        wide = SCALE * dot(ds_ref[a], keys_ref[a], 0, 0)
        for h in range(heads):
            wide_ref[h, pl.ds(pl.multiple_of(a * SPAN, 8), SPAN), :] = wide[h * SPAN : (h + 1) * SPAN]

    @pl.loop(0, heads // quad)
    def _(q):
        block = key_w[:, pl.ds(pl.multiple_of((step * (heads // quad) + q) * 16, 16), 16), :]
        parts = [
            dot(wide_ref[q * quad + h].astype(BF16), head_weight(block, h), 1, 0).astype(BF16)
            for h in range(quad)
        ]
        width = quad * HEAD_DIM
        o_ref[:, pl.ds(pl.multiple_of(q * width, width), width)] = jnp.concatenate(parts, axis=1)


def query_call(slots, here, ds, arrived, key_ring, groups):
    spans, kr, m_all = ds.shape
    ranks, _, enc = arrived.shape
    entries = slots.shape[0]
    m = m_all // groups
    heads = m // SPAN
    cols = heads * HEAD_DIM
    tok = spans * SPAN
    pieces = len(key_ring)
    anywhere = pl.BlockSpec(memory_space=pl.ANY)
    return pl.pallas_call(
        functools.partial(query_kernel, heads, pieces),
        grid_spec=pltpu.PrefetchScalarGridSpec(
            num_scalar_prefetch=2,
            grid=(groups,),
            in_specs=[pl.BlockSpec((spans, kr, m), lambda i, *_: (0, 0, i))] + [anywhere] * (1 + pieces),
            out_specs=pl.BlockSpec((tok, cols), lambda i, *_: (0, i)),
            scratch_shapes=[
                pltpu.VMEM((heads, tok, enc), F32),
                pltpu.VMEM((ranks,) + key_ring[0].shape[1:], BF16),
                pltpu.VMEM((spans, kr, enc), BF16),
                pltpu.SemaphoreType.DMA((pieces,)),
                pltpu.SemaphoreType.DMA((entries,)),
            ],
        ),
        out_shape=jax.ShapeDtypeStruct((tok, cols * groups), BF16),
        name="query_grad",
        cost_estimate=pl.CostEstimate(flops=3 * 10**9, bytes_accessed=12 * 10**6, transcendentals=0),
        compiler_params=pltpu.CompilerParams(vmem_limit_bytes=56 << 20),
    )(slots, here, ds, arrived, *key_ring)


def serve_kernel(table_ref, *refs):
    sources, (out_ref, sem) = refs[:-2], refs[-2:]
    steps = len(sources)
    here = table_ref[out_ref.shape[0]]
    copies = []
    for slot in range(out_ref.shape[0]):
        back = slot % steps
        row = jnp.where(here >= back, here - back, here - back + steps)
        block = jnp.maximum(table_ref[slot // steps * steps + row], 0)
        copies.append(pltpu.make_async_copy(sources[back].at[block], out_ref.at[slot], sem.at[slot]))
        copies[-1].start()
    for copy in copies:
        copy.wait()


def serve_call(table, sources):
    _, rows, enc = sources[0].shape
    slots = table.shape[0] - 1
    return pl.pallas_call(
        serve_kernel,
        in_specs=[pl.BlockSpec(memory_space=pltpu.SMEM)]
        + [pl.BlockSpec(memory_space=pl.ANY)] * len(sources),
        out_specs=pl.BlockSpec(memory_space=pltpu.VMEM),
        out_shape=jax.ShapeDtypeStruct((slots, rows, enc), BF16),
        scratch_shapes=[pltpu.SemaphoreType.DMA((slots,))],
        name="serve",
        cost_estimate=pl.CostEstimate(flops=0, bytes_accessed=8 * 10**6, transcendentals=0),
    )(table, *sources)


def pairs_x(groups, shift):
    return [(d, d // NX * NX + (d % NX + shift) % NX) for d in range(groups)]


def pairs_z(groups, shift):
    return [(d, (d + shift * NX) % groups) for d in range(groups)]


def tied(value, *others):
    return lax.optimization_barrier((value,) + others)[0]


def shards(queries, out_grad, key_weight, value_weight, encoded, nb_owner, nb_block):
    groups = lax.axis_size("dp")
    nz = groups // NX
    pipe = lax.axis_size("pipe")
    held, rows, enc = encoded.shape[1:]
    owners = nb_owner[0].reshape(-1)
    blocks = nb_block[0].reshape(-1)
    spans = nb_owner.shape[1]
    here, side = lax.axis_index("dp") // NX, lax.axis_index("dp") % NX
    over_x = [[z * NX + x for x in range(NX)] for z in range(nz)]

    def exchange(v, among=None):
        return lax.all_to_all(v, "dp", split_axis=0, concat_axis=0, tiled=True, axis_index_groups=among)

    def send_x(v, shift):
        return lax.ppermute(v, "dp", pairs_x(groups, shift))

    def send_z(v, shift):
        return lax.ppermute(v, "dp", pairs_z(groups, shift))

    def ring_move(ring):
        up, down = ring[-2:] if len(ring) > 1 else ring * 2
        if len(ring) == nz - 1:
            half = up.shape[0] // 2
            up, down = up[:half], down[half:]
        return ring + [send_z(up, 1), send_z(down, -1)]

    def pieces_of(weight):
        _, rows, _ = weight.shape
        cols = 4 * HEAD_DIM
        return weight.reshape(rows, -1, cols).swapaxes(0, 1).reshape(-1, cols)

    mine = jnp.stack([pieces_of(key_weight), pieces_of(value_weight)])
    row_weights = exchange(jnp.broadcast_to(mine[None], (NX,) + mine.shape), over_x)
    held_rows = ring_move([encoded[0]])
    held_rows[1:] = lax.optimization_barrier((held_rows[1], held_rows[2], row_weights))[:2]

    column_major = owners % NX * nz + owners // NX
    slot_ids = jnp.arange(groups, dtype=jnp.int32)[:, None]
    request = jnp.max(jnp.where(column_major[None, :] == slot_ids, blocks[None, :], -1), axis=1)
    by_column = jnp.broadcast_to(request.reshape(1, NX, nz), (nz, NX, nz)).reshape(groups, nz)
    asked = exchange(tied(by_column, row_weights))
    wanted = lax.dynamic_slice_in_dim(asked, here, 1, axis=1)[:, 0]
    row_wanted = lax.dynamic_slice_in_dim(asked, here * NX, NX, axis=0)

    keys, values = [row_weights[:, 0]], [row_weights[:, 1]]
    for _ in range(nz // 2 - 1):
        held_rows = ring_move(held_rows)
    for _ in range(nz // 2):
        keys, values = ring_move(keys), ring_move(values)
    far = jnp.concatenate(held_rows[-2:])
    in_order = held_rows[:1] + held_rows[1 : nz - 1 : 2] + [far] + held_rows[nz - 2 : 0 : -2]
    table = jnp.concatenate([row_wanted.reshape(-1), here[None]]).astype(jnp.int32)
    served = serve_call(table, in_order)
    arrived = exchange(served, over_x)
    incoming = lax.ppermute(out_grad, "pipe", [(s, (s - 1) % pipe) for s in range(pipe)])[0]

    slots = (owners % NX * nz + (here - owners // NX) % nz).astype(jnp.int32)
    hop_x, hop_z = (owners % NX - side) % NX, (owners // NX - here) % nz
    row_slot = (hop_x * nz + hop_z).astype(jnp.int32)
    first = jnp.argmax(owners[:, None] == owners[None, :], axis=1).astype(jnp.int32)
    by_side = jnp.take(row_wanted, (side - jnp.arange(NX)) % NX, axis=0)
    row_blocks = jnp.take(by_side, (here + jnp.arange(nz)) % nz, axis=1)
    at = here[None].astype(jnp.int32)
    slots, first, row_slot, wanted, row_blocks = lax.optimization_barrier(
        (slots, first, row_slot, wanted, row_blocks)
    )

    ds, dense, *parts = grads_call(
        slots, at, row_slot, owners, first, queries[0], incoming, arrived, keys, values, spans, 1
    )
    returned = exchange(dense)
    pieces = [parts[0]]
    for shift in range(1, NX):
        pieces.append(send_x(parts[shift], shift))
    query_grad = query_call(slots, at, ds, arrived, keys, 2)

    held_ids = jnp.arange(held, dtype=jnp.int32)
    row_sum = [jnp.zeros((nz, rows, enc // 2), F32)] * held
    for piece, of_piece in zip(pieces, row_blocks):
        for block in range(held):
            chosen = (of_piece == block).astype(F32)[:, None, None]
            row_sum[block] = row_sum[block] + chosen * piece.astype(F32)
    row_sum = jnp.stack(row_sum, axis=1).astype(BF16)
    left = row_sum[0].astype(F32)
    for shift in range(1, nz):
        left = left + send_z(row_sum[shift], shift).astype(F32)
    choose = (wanted[:, None] == held_ids[None, :]).astype(BF16)
    right = jnp.dot(choose.T, returned.reshape(groups, -1), preferred_element_type=F32)
    encoded_grad = jnp.concatenate([left, right.reshape(left.shape)], axis=-1)
    return query_grad[None], encoded_grad[None]


def solution(mesh):
    cut = P("pipe", "dp", None)
    deep = P("pipe", "dp", None, None)

    return jax.shard_map(
        shards,
        mesh=mesh,
        in_specs=(cut, cut, cut, cut, deep, cut, cut),
        out_specs=(cut, deep),
        check_vma=False,
    )
```
